32 devices in a mesh: seq: 16 (over z, x, core), tp: 2 (over y).
Axes of the slice: x: 2, y: 2, z: 4, core: 2. Of those that a mesh axis runs over, the one named last changes fastest.
Arguments:
- tokens: bfloat16 [8192, 4096], P('seq'), may hold values from -6 to 6
- w_in: bfloat16 [4096, 3, 4096], P('seq', None, 'tp'), may hold values from -0.09375 to 0.09375
- short_taps: float32 [3, 3, 4096], P(None, None, 'tp'), may hold values from -3 to 3
- decay_rate: float32 [256, 16], P('tp'), may hold values from 1.2207031e-05 to 0.04, as said below
- residue: float32 [256, 16], P('tp'), may hold values from -4 to 4
- skip_gain: float32 [4096], P('tp'), may hold values from -4 to 4
- w_out: bfloat16 [4096, 4096], P('tp'), may hold values from -0.125 to 0.125
Outputs:
- mixed: bfloat16 [8192, 4096], P('seq', 'tp')
The draws below stay inside these ranges and needn't reach their ends.
Inputs may be any that keep to these rules, and one draw needn't show every extreme that they name: `decay_rate`: every decay rate is positive.
All inputs are finite; a program needn't handle non-finite values.
Results may differ from the reference program's by a relative error of at most 0.0075.
Values may be sent and summed in bfloat16 or wider, within the bound.
A program may use at most 192 MiB of HBM per device.

```python
import math
import jax
import jax.numpy as jnp
from jax import lax

D = 4096
ORDER = 16
FILTER_WIDTH = 16
TAPS = 3
LENGTH = 8192
GROUPS = 256
N_TP = 2


def draw_decay_rate(key, part):
    first, second, third = jax.random.split(key, 3)
    share = 0.5
    coin = jax.random.uniform(first, (GROUPS, ORDER), jnp.float32) < share
    slow = jnp.exp(jax.random.uniform(second, (GROUPS, ORDER), jnp.float32, math.log(0.1 / LENGTH), math.log(2.0 / LENGTH)))
    fast = jnp.exp(jax.random.uniform(third, (GROUPS, ORDER), jnp.float32, math.log(0.01), math.log(0.04)))
    return jnp.clip(jnp.where(coin, fast, slow), 0.1 / LENGTH, 0.04).astype(jnp.float32)


def spiked(result, stream_key, source, target, blocks, factor):
    owner, partner = [(jnp.arange(result.shape[position]) // (result.shape[position] // blocks)).reshape([-1 if axis == position else 1 for axis in range(result.ndim)]) for position in (source, target)]
    chosen = jax.random.permutation(stream_key, blocks)[partner]
    strong = (owner == chosen) | (owner == (partner + blocks // 2) % blocks)
    return jnp.where(strong, factor * result, result)


def steps_of(own_key, extent, pieces, least, largest):
    gain = 1.0
    for position, shards_of in pieces:
        heights = jax.random.uniform(jax.random.fold_in(jax.random.fold_in(own_key, 6), position), (shards_of,), jnp.float32, least / len(pieces), largest / len(pieces))
        gain = gain * jnp.repeat(jnp.exp(heights), extent[position] // shards_of).reshape((-1,) + (1,) * (len(extent) - 1 - position))
    return gain


def gaussian(own_key, extent, width, limit, pieces=(), held_as=jnp.bfloat16):
    level = steps_of(own_key, extent, pieces, -0.22, 0.18) if pieces else 1.0
    array = jax.random.normal(own_key, extent, jnp.float32) * width * level
    return jnp.minimum(jnp.maximum(array, -limit), limit).astype(held_as)


def gaussian_with(rng, extent, spread, bound, cuts, heavy, kind=jnp.bfloat16):
    values = spread * jax.random.normal(rng, extent, jnp.float32)
    if cuts:
        values = values * steps_of(rng, extent, cuts, -0.22, 0.18)
    return jnp.clip(spiked(values, jax.random.fold_in(rng, 3), *heavy), -bound, bound).astype(kind)


def setup_inputs(seed: int = 0) -> dict:
    arg_keys = jax.random.split(jax.random.key(seed), 8)
    return {
        "tokens": gaussian(arg_keys[0], (LENGTH, D), 1.0, 6.0, ((0, 16),)),
        "w_in": gaussian(arg_keys[1], (D, 3, D), D ** -0.5, 0.09375, ((0, 16), (2, 2))),
        "short_taps": gaussian(arg_keys[2], (TAPS, 3, D), 0.6, 3.0, ((2, 2),), jnp.float32),
        "decay_rate": draw_decay_rate(jax.random.fold_in(arg_keys[7], 71), 0),
        "residue": gaussian(arg_keys[4], (GROUPS, ORDER), 1.0, 4.0, ((0, 2),), jnp.float32),
        "skip_gain": gaussian(arg_keys[5], (D,), 1.0, 4.0, ((0, 2),), jnp.float32),
        "w_out": gaussian_with(arg_keys[6], (D, D), D ** -0.5, 0.125, ((0, 2),), (0, 1, 2, 2.0)),
    }


def reference(tokens, w_in, short_taps, decay_rate, residue, skip_gain, w_out):
    proj = jnp.dot(tokens, w_in.reshape(D, 3 * D), preferred_element_type=jnp.float32)
    proj = proj.astype(jnp.bfloat16).reshape(LENGTH, 3, D).astype(jnp.float32)
    padded = jnp.concatenate([jnp.zeros((TAPS - 1, 3, D), jnp.float32), proj], axis=0)
    filtered = jnp.zeros((LENGTH, 3, D), jnp.float32)
    for tap in range(TAPS):
        filtered = filtered + short_taps[tap] * padded[TAPS - 1 - tap:TAPS - 1 - tap + LENGTH]
    query = filtered[:, 0]
    gated = filtered[:, 1] * filtered[:, 2]
    decay = jnp.repeat(jnp.exp(-decay_rate), FILTER_WIDTH, axis=0).T
    weight_mode = jnp.repeat(residue * jnp.sqrt(2.0 * decay_rate / ORDER), FILTER_WIDTH, axis=0).T

    def advance(state, value):
        state = decay * state + value[None, :]
        return (state, lax.optimization_barrier(jnp.sum(weight_mode * state, axis=0)))
    _, conv = lax.scan(advance, jnp.zeros((ORDER, D), jnp.float32), gated)
    mix = (query * (conv + skip_gain * gated)).astype(jnp.bfloat16)
    share = D // N_TP
    total = jnp.zeros((LENGTH, D), jnp.float32)
    for block in range(N_TP):
        partial_value = jnp.dot(mix[:, block * share:(block + 1) * share], w_out[block * share:(block + 1) * share], preferred_element_type=jnp.float32)
        partial_value = lax.optimization_barrier(partial_value.astype(jnp.bfloat16))
        total = total + partial_value.astype(jnp.float32)
    return total.astype(jnp.bfloat16)
```

```python
import functools

import jax
import jax.numpy as jnp
from jax import lax
from jax.experimental import pallas as pl
from jax.experimental.pallas import tpu as pltpu
from jax.sharding import PartitionSpec as P

SUB = 128
LANES = 256
CHUNK = 512
HALO = 16
MESH = pl.DeviceIdType.MESH
HIGHEST = lax.Precision.HIGHEST


def shifted_by(block, axis, distance):
    devices = range(lax.axis_size(axis))
    route = [(i - distance, i) for i in devices if i - distance in devices]
    return lax.ppermute(block, axis, route)


def rotated(block, axis, distance):
    size = lax.axis_size(axis)
    return lax.ppermute(block, axis, [(i, (i + distance) % size) for i in range(size)])


def fanned(state, width, order):
    lanes = state.shape[1]
    tile = lanes // width
    full = jnp.concatenate([state] * tile, axis=0)
    row = lax.broadcasted_iota(jnp.int32, full.shape, 0) // order
    lane = lax.broadcasted_iota(jnp.int32, full.shape, 1) // width
    return jnp.where(row == lane, full, 0.0)


def conv_kernel(
    width, q_ref, k_ref, v_ref, taps_ref, toep_ref, leave_ref, reach_ref, fade_ref, skip_ref,
    query_ref, base_ref, state_ref
):
    taps = taps_ref.shape[0]
    count, lanes = query_ref.shape
    order = state_ref.shape[0]
    tile = lanes // width

    def filtered(ref, which):
        value = ref[...].astype(jnp.float32)
        total = None
        for tap in range(taps):
            term = taps_ref[tap, which][None, :] * value[HALO - tap : HALO - tap + count]
            total = term if total is None else total + term
        return total

    query_ref[...] = filtered(q_ref, 0)
    gated = filtered(k_ref, 1) * filtered(v_ref, 2)
    lane = lax.broadcasted_iota(jnp.int32, (SUB, lanes), 1) // width
    row = lax.broadcasted_iota(jnp.int32, (tile * order, lanes), 0) // order
    diagonal = row == lax.broadcasted_iota(jnp.int32, (tile * order, lanes), 1) // width
    toep = toep_ref[...].reshape(tile * SUB, SUB)
    state = jnp.zeros((tile * order, lanes), jnp.float32)
    for block in range(count // SUB):
        piece = gated[block * SUB : (block + 1) * SUB]
        wide = jnp.dot(toep, piece.astype(jnp.bfloat16), preferred_element_type=jnp.float32)
        local = skip_ref[...] * piece
        picked = wide[:SUB]
        for g in range(1, tile):
            picked = jnp.where(lane == g, wide[g * SUB : (g + 1) * SUB], picked)
        local = local + picked
        if block:
            local = local + jnp.dot(
                reach_ref[:SUB], state, precision=HIGHEST, preferred_element_type=jnp.float32
            )
        base_ref[block * SUB : (block + 1) * SUB] = local
        fresh = jnp.dot(
            leave_ref[...], piece, precision=HIGHEST, preferred_element_type=jnp.float32
        )
        state = fade_ref[...] * state + jnp.where(diagonal, fresh, 0.0)
    compact = state[:order]
    for g in range(1, tile):
        compact = compact + state[g * order : (g + 1) * order]
    state_ref[...] = compact


def convolved(proj, taps, toep, leave, reach, fade, skip, width, order, count):
    chans = skip.shape[1]
    lanes = min(LANES, chans)
    steps = chans // lanes
    tile = lanes // width
    rows = proj.shape[0]
    return pl.pallas_call(
        functools.partial(conv_kernel, width),
        grid=(steps,),
        in_specs=[
            pl.BlockSpec((rows, lanes), lambda i: (0, i)),
            pl.BlockSpec((rows, lanes), lambda i: (0, steps + i)),
            pl.BlockSpec((rows, lanes), lambda i: (0, 2 * steps + i)),
            pl.BlockSpec((taps.shape[0], 3, lanes), lambda i: (0, 0, i)),
            pl.BlockSpec((tile, SUB, SUB), lambda i: (i, 0, 0)),
            pl.BlockSpec((tile * order, SUB), lambda i: (i, 0)),
            pl.BlockSpec((count, tile * order), lambda i: (0, i)),
            pl.BlockSpec((tile * order, 1), lambda i: (i, 0)),
            pl.BlockSpec((1, lanes), lambda i: (0, i)),
        ],
        out_specs=[
            pl.BlockSpec((count, lanes), lambda i: (0, i)),
            pl.BlockSpec((count, lanes), lambda i: (0, i)),
            pl.BlockSpec((order, lanes), lambda i: (0, i)),
        ],
        out_shape=[
            jax.ShapeDtypeStruct((count, chans), jnp.float32),
            jax.ShapeDtypeStruct((count, chans), jnp.float32),
            jax.ShapeDtypeStruct((order, chans), jnp.float32),
        ],
        cost_estimate=pl.CostEstimate(
            flops=2 * count * chans * SUB * tile, bytes_accessed=count * chans * 20, transcendentals=0
        ),
        name="conv",
    )(proj, proj, proj, taps, toep, leave, reach, fade, skip)


def share_kernel(own_ref, all_ref, send_sems, recv_sems):
    size = all_ref.shape[0]
    here = lax.axis_index("seq")
    barrier = pltpu.get_barrier_semaphore()
    for d in range(1, size):
        pl.semaphore_signal(
            barrier, inc=1, device_id={"seq": lax.rem(here + d, size)}, device_id_type=MESH
        )
    pl.semaphore_wait(barrier, size - 1)
    copies = []
    for d in range(1, size):
        copy = pltpu.make_async_remote_copy(
            src_ref=own_ref,
            dst_ref=all_ref.at[here],
            send_sem=send_sems.at[d - 1],
            recv_sem=recv_sems.at[d - 1],
            device_id={"seq": lax.rem(here + d, size)},
            device_id_type=MESH,
        )
        copy.start()
        copies.append(copy)
    all_ref[here] = own_ref[...]
    for copy in copies:
        copy.wait()


def shared(state):
    size = lax.axis_size("seq")
    return pl.pallas_call(
        share_kernel,
        out_shape=jax.ShapeDtypeStruct((size,) + state.shape, state.dtype),
        in_specs=[pl.BlockSpec(memory_space=pltpu.VMEM)],
        out_specs=pl.BlockSpec(memory_space=pltpu.VMEM),
        scratch_shapes=[
            pltpu.SemaphoreType.DMA((size - 1,)),
            pltpu.SemaphoreType.DMA((size - 1,)),
        ],
        compiler_params=pltpu.CompilerParams(collective_id=0, has_side_effects=True),
        cost_estimate=pl.CostEstimate(
            flops=0, bytes_accessed=40 * size * state.size, transcendentals=0
        ),
        name="share",
    )(state)


def mix_kernel(width, query_ref, base_ref, all_ref, weight_ref, reach_ref, mix_ref):
    order = all_ref.shape[1]
    entering = jnp.sum(all_ref[...] * weight_ref[...], axis=0)
    carried = jnp.dot(
        reach_ref[...],
        fanned(entering, width, order),
        precision=HIGHEST,
        preferred_element_type=jnp.float32,
    )
    mix_ref[...] = (query_ref[...] * (base_ref[...] + carried)).astype(mix_ref.dtype)


def mixed_of(query, base, everything, weight, reach, width):
    count, chans = query.shape
    size, order, _ = everything.shape
    lanes = min(LANES, chans)
    cols = lanes // width * order
    return pl.pallas_call(
        functools.partial(mix_kernel, width),
        grid=(chans // lanes,),
        in_specs=[
            pl.BlockSpec((count, lanes), lambda i: (0, i)),
            pl.BlockSpec((count, lanes), lambda i: (0, i)),
            pl.BlockSpec((size, order, lanes), lambda i: (0, 0, i)),
            pl.BlockSpec((size, order, lanes), lambda i: (0, 0, i)),
            pl.BlockSpec((count, cols), lambda i: (0, i)),
        ],
        out_specs=pl.BlockSpec((count, lanes), lambda i: (0, i)),
        out_shape=jax.ShapeDtypeStruct((count, chans), jnp.bfloat16),
        cost_estimate=pl.CostEstimate(
            flops=12 * count * chans * cols, bytes_accessed=count * chans * 10, transcendentals=0
        ),
        name="mix",
    )(query, base, everything, weight, reach)


def shards(tokens, w_in, short_taps, decay_rate, residue, skip_gain, w_out):
    count = tokens.shape[0]
    chans = w_in.shape[2]
    groups, order = decay_rate.shape
    width = chans // groups
    taps = short_taps.shape[0]
    size, here = lax.axis_size("seq"), lax.axis_index("seq")
    n_tp, part = lax.axis_size("tp"), lax.axis_index("tp")
    chunk = min(CHUNK, chans)
    chunks = chans // chunk

    pieces = []
    for c in range(chunks):
        cols = w_in[:, :, c * chunk : (c + 1) * chunk].reshape(w_in.shape[0], 3 * chunk)
        pieces.append(lax.all_gather(cols, "seq", axis=0, tiled=True))

    before = shifted_by(tokens[count - (taps - 1) :], "seq", 1)
    extended = jnp.concatenate(
        [jnp.zeros((HALO - (taps - 1), tokens.shape[1]), tokens.dtype), before, tokens], axis=0
    )

    out_cols = w_out.shape[1] // n_tp

    def columns_for(target):
        return lax.dynamic_slice_in_dim(w_out, target * out_cols, out_cols, axis=1)

    outs = [columns_for(part)]
    for d in range(1, n_tp):
        outs.append(rotated(columns_for((part + d) % n_tp), "tp", d))

    weight_mode = residue * jnp.sqrt(2.0 * decay_rate / order)
    offsets = jnp.arange(SUB, dtype=jnp.float32)
    kernel = jnp.einsum(
        "gm,gmd->gd",
        weight_mode,
        jnp.exp(-decay_rate[:, :, None] * offsets[None, None, :]),
        precision=HIGHEST,
    )
    lag = jnp.arange(SUB)[:, None] - jnp.arange(SUB)[None, :]
    toep = jnp.where(lag[None] >= 0, kernel[:, jnp.maximum(lag, 0)], 0.0).astype(jnp.bfloat16)
    rate = decay_rate.reshape(groups * order)
    leave = jnp.exp(-rate[:, None] * (SUB - 1.0 - offsets[None, :]))
    fade = jnp.exp(-rate * SUB)[:, None]
    positions = jnp.arange(count, dtype=jnp.float32)
    reach = weight_mode.reshape(groups * order)[None] * jnp.exp(
        -rate[None] * (positions[:, None] + 1.0)
    )
    by_mode = jnp.repeat(decay_rate.T, width, axis=1)
    ahead = (here - 1 - jnp.arange(size))[:, None, None]
    weight = jnp.where(
        ahead >= 0, jnp.exp(-by_mode[None] * (count * jnp.maximum(ahead, 0).astype(jnp.float32))), 0.0
    )
    skip = skip_gain[None]

    total = jnp.zeros((count, out_cols), jnp.float32)
    for c in range(chunks):
        lane = slice(c * chunk, (c + 1) * chunk)
        mode = slice(c * chunk // width * order, (c + 1) * chunk // width * order)
        group = slice(c * chunk // width, (c + 1) * chunk // width)
        proj = jnp.dot(extended, pieces[c], preferred_element_type=jnp.float32).astype(jnp.bfloat16)
        query, base, final = convolved(
            proj, short_taps[:, :, lane], toep[group], leave[mode], reach[:, mode], fade[mode],
            skip[:, lane], width, order, count,
        )
        everything = shared(final)
        mix = mixed_of(query, base, everything, weight[:, :, lane], reach[:, mode], width)
        for d in range(n_tp):
            block = mix if d == 0 else rotated(mix, "tp", d)
            total = total + jnp.dot(block, outs[d][lane], preferred_element_type=jnp.float32)
    return total.astype(jnp.bfloat16)


def solution(mesh):
    in_specs = (
        P("seq", None),
        P("seq", None, "tp"),
        P(None, None, "tp"),
        P("tp", None),
        P("tp", None),
        P("tp"),
        P("tp", None),
    )
    out_specs = P("seq", "tp")
    return jax.shard_map(shards, mesh=mesh, in_specs=in_specs, out_specs=out_specs, check_vma=False)
```

```python
import functools

import jax
import jax.numpy as jnp
from jax import lax
from jax.experimental import pallas as pl
from jax.experimental.pallas import tpu as pltpu
from jax.sharding import PartitionSpec as P

SUB = 128
LANES = 256
HALO = 16
MESH = pl.DeviceIdType.MESH
HIGHEST = lax.Precision.HIGHEST


def shifted_by(block, axis, distance):
    devices = range(lax.axis_size(axis))
    route = [(i - distance, i) for i in devices if i - distance in devices]
    return lax.ppermute(block, axis, route)


def rotated(block, axis, distance):
    size = lax.axis_size(axis)
    return lax.ppermute(block, axis, [(i, (i + distance) % size) for i in range(size)])


def fanned(state, width, order):
    lanes = state.shape[1]
    tile = lanes // width
    full = jnp.concatenate([state] * tile, axis=0)
    row = lax.broadcasted_iota(jnp.int32, full.shape, 0) // order
    lane = lax.broadcasted_iota(jnp.int32, full.shape, 1) // width
    return jnp.where(row == lane, full, 0.0)


def conv_kernel(
    width, q_ref, k_ref, v_ref, taps_ref, toep_ref, leave_ref, reach_ref, fade_ref, skip_ref,
    query_ref, base_ref, state_ref
):
    taps = taps_ref.shape[0]
    count, lanes = query_ref.shape
    order = state_ref.shape[0]
    tile = lanes // width

    def filtered(ref, which):
        value = ref[...].astype(jnp.float32)
        total = None
        for tap in range(taps):
            term = taps_ref[tap, which][None, :] * value[HALO - tap : HALO - tap + count]
            total = term if total is None else total + term
        return total

    query_ref[...] = filtered(q_ref, 0)
    gated = filtered(k_ref, 1) * filtered(v_ref, 2)
    lane = lax.broadcasted_iota(jnp.int32, (SUB, lanes), 1) // width
    row = lax.broadcasted_iota(jnp.int32, (tile * order, lanes), 0) // order
    diagonal = row == lax.broadcasted_iota(jnp.int32, (tile * order, lanes), 1) // width
    toep = toep_ref[...].reshape(tile * SUB, SUB)
    state = jnp.zeros((tile * order, lanes), jnp.float32)
    for block in range(count // SUB):
        piece = gated[block * SUB : (block + 1) * SUB]
        wide = jnp.dot(toep, piece.astype(jnp.bfloat16), preferred_element_type=jnp.float32)
        local = skip_ref[...] * piece
        picked = wide[:SUB]
        for g in range(1, tile):
            picked = jnp.where(lane == g, wide[g * SUB : (g + 1) * SUB], picked)
        local = local + picked
        if block:
            local = local + jnp.dot(
                reach_ref[:SUB], state, precision=HIGHEST, preferred_element_type=jnp.float32
            )
        base_ref[block * SUB : (block + 1) * SUB] = local
        fresh = jnp.dot(
            leave_ref[...], piece, precision=HIGHEST, preferred_element_type=jnp.float32
        )
        state = fade_ref[...] * state + jnp.where(diagonal, fresh, 0.0)
    compact = state[:order]
    for g in range(1, tile):
        compact = compact + state[g * order : (g + 1) * order]
    state_ref[...] = compact


def convolved(proj, taps, toep, leave, reach, fade, skip, width, order, count):
    chans = skip.shape[1]
    lanes = min(LANES, chans)
    steps = chans // lanes
    tile = lanes // width
    segments, rows, _ = proj.shape
    return pl.pallas_call(
        functools.partial(conv_kernel, width),
        grid=(steps, segments),
        in_specs=[
            pl.BlockSpec((None, rows, lanes), lambda i, j: (j, 0, i)),
            pl.BlockSpec((None, rows, lanes), lambda i, j: (j, 0, steps + i)),
            pl.BlockSpec((None, rows, lanes), lambda i, j: (j, 0, 2 * steps + i)),
            pl.BlockSpec((taps.shape[0], 3, lanes), lambda i, j: (0, 0, i)),
            pl.BlockSpec((tile, SUB, SUB), lambda i, j: (i, 0, 0)),
            pl.BlockSpec((tile * order, SUB), lambda i, j: (i, 0)),
            pl.BlockSpec((count, tile * order), lambda i, j: (0, i)),
            pl.BlockSpec((tile * order, 1), lambda i, j: (i, 0)),
            pl.BlockSpec((1, lanes), lambda i, j: (0, i)),
        ],
        out_specs=[
            pl.BlockSpec((None, count, lanes), lambda i, j: (j, 0, i)),
            pl.BlockSpec((None, count, lanes), lambda i, j: (j, 0, i)),
            pl.BlockSpec((None, order, lanes), lambda i, j: (j, 0, i)),
        ],
        out_shape=[
            jax.ShapeDtypeStruct((segments, count, chans), jnp.float32),
            jax.ShapeDtypeStruct((segments, count, chans), jnp.float32),
            jax.ShapeDtypeStruct((segments, order, chans), jnp.float32),
        ],
        cost_estimate=pl.CostEstimate(
            flops=2 * count * chans * SUB * tile, bytes_accessed=count * chans * 20, transcendentals=0
        ),
        name="conv",
    )(proj, proj, proj, taps, toep, leave, reach, fade, skip)


def place():
    size, here = lax.axis_size("seq"), lax.axis_index("seq")
    return here // 4, lax.rem(here // 2, 2), lax.rem(here, 2), size // 4


def index_of(z, x, core):
    return z * 4 + x * 2 + core


def greet(peers):
    barrier = pltpu.get_barrier_semaphore()
    for peer in peers:
        pl.semaphore_signal(barrier, inc=1, device_id=peer, device_id_type=MESH)
    pl.semaphore_wait(barrier, len(peers))


def remote(source, target, send_sem, recv_sem, peer):
    return pltpu.make_async_remote_copy(
        src_ref=source,
        dst_ref=target,
        send_sem=send_sem,
        recv_sem=recv_sem,
        device_id=peer,
        device_id_type=MESH,
    )


def gather_kernel(
    own_ref, pieces_ref, tok_ref, w_ref, local_sems,
    line_send, line_recv, pass_send, pass_recv, pair_send, pair_recv,
    tp_send, tp_recv, core_send, core_recv, early_send, early_recv,
):
    z, x, core, depth = place()
    parity = lax.rem(z, 2)
    mate = z + 1 - 2 * parity
    n_tp, part = lax.axis_size("tp"), lax.axis_index("tp")
    cols = own_ref.shape[1] // n_tp
    mine = index_of(z, x, core)
    side = {"seq": index_of(z, 1 - x, core)}
    twin = {"seq": index_of(z, x, 1 - core)}
    pair = {"seq": index_of(mate, x, core)}

    def on_line(step, other, sign):
        there = lax.rem(z + sign * step + depth, depth)
        return there, (1 - core if other else core)

    hops = [(step, other) for step in range(depth) for other in range(2)][1:]
    hops = sorted(hops, key=lambda hop: (min(hop[0], depth - hop[0]), hop))
    peers = [side]
    for hop in hops:
        there, which = on_line(*hop, 1)
        peers.append({"seq": index_of(there, x, which)})
    tps = [{"tp": lax.rem(part + d, n_tp)} for d in range(1, n_tp)]
    greet(peers + tps)

    def band(which):
        return pl.ds(pl.multiple_of(which * cols, cols), cols)

    own_slot, mate_slot = 2 * parity + core, 2 * (1 - parity) + core
    role = own_slot
    stay = [
        pltpu.make_async_copy(own_ref, tok_ref.at[own_slot], local_sems.at[0]),
        pltpu.make_async_copy(pieces_ref.at[role], w_ref.at[mine], local_sems.at[1]),
    ]
    for copy in stay:
        copy.start()
    started = []

    def begin(copy):
        copy.start()
        started.append(copy)
        return copy

    first = begin(remote(
        pieces_ref.at[role], w_ref.at[mine], pass_send.at[0], pass_recv.at[0], side
    ))
    line = {}
    paired = None
    for n, hop in enumerate(hops):
        if n == 4 or (n == len(hops) - 1 and paired is None):
            paired = begin(remote(
                own_ref.at[:, band(part)], tok_ref.at[own_slot, :, band(part)],
                pair_send, pair_recv, pair,
            ))
        there, which = on_line(*hop, 1)
        index = 2 * hop[0] + hop[1]
        line[hop] = begin(remote(
            pieces_ref.at[2 * lax.rem(there, 2) + which], w_ref.at[mine],
            line_send.at[index], line_recv.at[index], {"seq": index_of(there, x, which)},
        ))
    early = begin(remote(own_ref, tok_ref.at[own_slot], early_send, early_recv, twin))

    forwards = []

    def hand_on(hop):
        index = 2 * hop[0] + hop[1]
        there, which = on_line(*hop, -1)
        source = index_of(there, x, which)
        line[hop].wait_recv()
        forwards.append(begin(remote(
            w_ref.at[source], w_ref.at[source], pass_send.at[index], pass_recv.at[index], side
        )))

    def to_twin(which, slot):
        return begin(remote(
            tok_ref.at[mate_slot, :, band(which)], tok_ref.at[mate_slot, :, band(which)],
            core_send.at[slot], core_recv.at[slot], twin,
        ))

    for hop in hops[:4]:
        hand_on(hop)
    paired.wait_recv()
    across = []
    for d in range(1, n_tp):
        across.append(begin(remote(
            tok_ref.at[mate_slot, :, band(part)], tok_ref.at[mate_slot, :, band(part)],
            tp_send.at[d - 1], tp_recv.at[d - 1], tps[d - 1],
        )))
    twins = [to_twin(part, 0)]
    for hop in hops[4:]:
        hand_on(hop)
    for d in range(1, n_tp):
        across[d - 1].wait_recv()
        twins.append(to_twin(lax.rem(part - d + n_tp, n_tp), d))
    for copy in [first, early] + forwards + twins:
        copy.wait_recv()
    for copy in started:
        copy.wait_send()
    for copy in stay:
        copy.wait()


def gathered(own, pieces):
    size, n_tp = lax.axis_size("seq"), lax.axis_size("tp")
    line = size // 2
    anywhere = pl.BlockSpec(memory_space=pl.ANY)
    one = pltpu.SemaphoreType.DMA(())
    return pl.pallas_call(
        gather_kernel,
        out_shape=[
            jax.ShapeDtypeStruct((4,) + own.shape, own.dtype),
            jax.ShapeDtypeStruct((size,) + pieces.shape[1:], pieces.dtype),
        ],
        in_specs=[anywhere, anywhere],
        out_specs=[anywhere, anywhere],
        scratch_shapes=[
            pltpu.SemaphoreType.DMA((2,)),
            pltpu.SemaphoreType.DMA((line,)),
            pltpu.SemaphoreType.DMA((line,)),
            pltpu.SemaphoreType.DMA((line,)),
            pltpu.SemaphoreType.DMA((line,)),
            one,
            one,
            pltpu.SemaphoreType.DMA((n_tp,)),
            pltpu.SemaphoreType.DMA((n_tp,)),
            pltpu.SemaphoreType.DMA((n_tp,)),
            pltpu.SemaphoreType.DMA((n_tp,)),
            one,
            one,
        ],
        compiler_params=pltpu.CompilerParams(collective_id=0, has_side_effects=True),
        name="gather",
    )(own, pieces)


def share_kernel(own_ref, all_ref, send_sems, recv_sems):
    total = all_ref.shape[0]
    z, x, core, depth = place()
    here = (z // 2) * 2 + x

    def peer(d):
        there = lax.rem(here + d, total)
        return {"seq": index_of(2 * (there // 2) + lax.rem(z, 2), lax.rem(there, 2), core)}

    peers = [peer(d) for d in range(1, total)]
    greet(peers)
    copies = []
    for d in range(1, total):
        copy = remote(
            own_ref, all_ref.at[here], send_sems.at[d - 1], recv_sems.at[d - 1], peers[d - 1]
        )
        copy.start()
        copies.append(copy)
    all_ref[here] = own_ref[...]
    for copy in copies:
        copy.wait()


def shared(state):
    total = lax.axis_size("seq") // 4
    return pl.pallas_call(
        share_kernel,
        out_shape=jax.ShapeDtypeStruct((total,) + state.shape, state.dtype),
        in_specs=[pl.BlockSpec(memory_space=pltpu.VMEM)],
        out_specs=pl.BlockSpec(memory_space=pltpu.VMEM),
        scratch_shapes=[
            pltpu.SemaphoreType.DMA((total - 1,)),
            pltpu.SemaphoreType.DMA((total - 1,)),
        ],
        compiler_params=pltpu.CompilerParams(collective_id=1, has_side_effects=True),
        name="share",
    )(state)


def spread_kernel(mix_ref, full_ref, local_sem, send_sems, recv_sems):
    z, x, core, _ = place()
    parity = lax.rem(z, 2)
    me = 2 * parity + core
    base = 2 * (z // 2)

    def peer(d):
        there = lax.rem(me + d, 4)
        return there, {"seq": index_of(base + there // 2, x, lax.rem(there, 2))}

    greet([peer(d)[1] for d in range(1, 4)])
    copies = []
    for d in (2, 1, 3):
        there, device = peer(d)
        copy = remote(
            mix_ref.at[there], full_ref.at[me], send_sems.at[d - 1], recv_sems.at[d - 1], device
        )
        copy.start()
        copies.append(copy)
    stay = pltpu.make_async_copy(mix_ref.at[me], full_ref.at[me], local_sem)
    stay.start()
    for copy in copies:
        copy.wait()
    stay.wait()


def spread(mix):
    return pl.pallas_call(
        spread_kernel,
        out_shape=jax.ShapeDtypeStruct(mix.shape, mix.dtype),
        in_specs=[pl.BlockSpec(memory_space=pltpu.VMEM)],
        out_specs=pl.BlockSpec(memory_space=pltpu.VMEM),
        scratch_shapes=[
            pltpu.SemaphoreType.DMA(()),
            pltpu.SemaphoreType.DMA((3,)),
            pltpu.SemaphoreType.DMA((3,)),
        ],
        compiler_params=pltpu.CompilerParams(collective_id=2, has_side_effects=True),
        name="spread",
    )(mix)


def mix_kernel(width, query_ref, base_ref, all_ref, weight_ref, reach_ref, mix_ref):
    order = all_ref.shape[1]
    entering = jnp.sum(all_ref[...] * weight_ref[...], axis=0)
    carried = jnp.dot(
        reach_ref[...],
        fanned(entering, width, order),
        precision=HIGHEST,
        preferred_element_type=jnp.float32,
    )
    mix_ref[...] = (query_ref[...] * (base_ref[...] + carried)).astype(mix_ref.dtype)


def mixed_of(query, base, everything, weight, reach, width):
    segments, count, chans = query.shape
    size, order, _ = everything.shape
    lanes = min(LANES, chans)
    cols = lanes // width * order
    return pl.pallas_call(
        functools.partial(mix_kernel, width),
        grid=(chans // lanes, segments),
        in_specs=[
            pl.BlockSpec((None, count, lanes), lambda i, j: (j, 0, i)),
            pl.BlockSpec((None, count, lanes), lambda i, j: (j, 0, i)),
            pl.BlockSpec((size, order, lanes), lambda i, j: (0, 0, i)),
            pl.BlockSpec((None, size, order, lanes), lambda i, j: (j, 0, 0, i)),
            pl.BlockSpec((count, cols), lambda i, j: (0, i)),
        ],
        out_specs=pl.BlockSpec((None, count, lanes), lambda i, j: (j, 0, i)),
        out_shape=jax.ShapeDtypeStruct((segments, count, chans), jnp.bfloat16),
        name="mix",
    )(query, base, everything, weight, reach)


def shards(tokens, w_in, short_taps, decay_rate, residue, skip_gain, w_out):
    count = tokens.shape[0]
    rows, _, all_chans = w_in.shape
    width = all_chans // decay_rate.shape[0]
    taps = short_taps.shape[0]
    z, x, core, depth = place()
    parity = lax.rem(z, 2)
    role = 2 * parity + core
    n_tp, part = lax.axis_size("tp"), lax.axis_index("tp")
    chans = all_chans // 4

    before = shifted_by(tokens[count - (taps - 1) :], "seq", 1)
    extended = jnp.concatenate(
        [jnp.zeros((HALO - (taps - 1), tokens.shape[1]), tokens.dtype), before, tokens], axis=0
    )
    pieces = w_in.reshape(rows, 3, 4, chans).transpose(2, 0, 1, 3).reshape(4, rows, 3 * chans)
    tok, weights = gathered(extended, pieces)

    def own(array, axis):
        share = array.shape[axis] // 4
        return lax.dynamic_slice_in_dim(array, role * share, share, axis)

    short_taps, skip = own(short_taps, 2), own(skip_gain[None], 1)
    decay_rate, residue = own(decay_rate, 0), own(residue, 0)
    groups, order = decay_rate.shape
    weight_mode = residue * jnp.sqrt(2.0 * decay_rate / order)
    offsets = jnp.arange(SUB, dtype=jnp.float32)
    kernel = jnp.einsum(
        "gm,gmd->gd",
        weight_mode,
        jnp.exp(-decay_rate[:, :, None] * offsets[None, None, :]),
        precision=HIGHEST,
    )
    lag = jnp.arange(SUB)[:, None] - jnp.arange(SUB)[None, :]
    toep = jnp.where(lag[None] >= 0, kernel[:, jnp.maximum(lag, 0)], 0.0).astype(jnp.bfloat16)
    rate = decay_rate.reshape(groups * order)
    leave = jnp.exp(-rate[:, None] * (SUB - 1.0 - offsets[None, :]))
    fade = jnp.exp(-rate * SUB)[:, None]
    positions = jnp.arange(count, dtype=jnp.float32)
    reach = weight_mode.reshape(groups * order)[None] * jnp.exp(
        -rate[None] * (positions[:, None] + 1.0)
    )
    by_mode = jnp.repeat(decay_rate.T, width, axis=1)
    slot = jnp.arange(4)
    own_block = index_of(2 * (z // 2) + slot // 2, x, slot % 2)
    team = jnp.arange(depth)[:, None]
    other_block = index_of(2 * (team // 2) + slot[None] // 2, team % 2, slot[None] % 2).reshape(-1)
    ahead = (own_block[:, None] - 1 - other_block[None, :])[:, :, None, None]
    weight = jnp.where(
        ahead >= 0, jnp.exp(-by_mode * (count * jnp.maximum(ahead, 0).astype(jnp.float32))), 0.0
    )

    proj = jnp.dot(
        tok.reshape(-1, tok.shape[2]),
        weights.reshape(-1, weights.shape[2]),
        preferred_element_type=jnp.float32,
    ).astype(jnp.bfloat16).reshape(4, -1, 3 * chans)
    query, base, final = convolved(
        proj, short_taps, toep, leave, reach, fade, skip, width, order, count
    )
    everything = shared(final).reshape(-1, order, chans)
    mix = spread(mixed_of(query, base, everything, weight, reach, width))
    full = mix.transpose(1, 0, 2).reshape(count, 4 * chans)

    share = w_out.shape[1] // n_tp
    half = share // 2

    def product(target, piece):
        cols = lax.dynamic_slice_in_dim(w_out, target * share + piece * half, half, axis=1)
        return jnp.dot(full, cols, preferred_element_type=jnp.float32).astype(jnp.bfloat16)

    arrived = []
    for d in range(1, n_tp):
        for piece in range(2):
            arrived.append(rotated(product((part + d) % n_tp, piece), "tp", d))
    results = []
    for piece in range(2):
        total = product(part, piece).astype(jnp.float32)
        for d in range(1, n_tp):
            total = total + arrived[2 * (d - 1) + piece].astype(jnp.float32)
        results.append(total.astype(jnp.bfloat16))
    return jnp.concatenate(results, axis=1)


def solution(mesh):
    in_specs = (
        P("seq", None),
        P("seq", None, "tp"),
        P(None, None, "tp"),
        P("tp", None),
        P("tp", None),
        P("tp"),
        P("tp", None),
    )
    out_specs = P("seq", "tp")
    return jax.shard_map(shards, mesh=mesh, in_specs=in_specs, out_specs=out_specs, check_vma=False)
```

```python
import functools

import jax
import jax.numpy as jnp
from jax import lax
from jax.experimental import pallas as pl
from jax.experimental.pallas import tpu as pltpu
from jax.sharding import PartitionSpec as P

SUB = 128
LANES = 256
HALO = 16
MESH = pl.DeviceIdType.MESH
HIGHEST = lax.Precision.HIGHEST


def shifted_by(block, axis, distance):
    devices = range(lax.axis_size(axis))
    route = [(i - distance, i) for i in devices if i - distance in devices]
    return lax.ppermute(block, axis, route)


def fanned(state, width, order):
    lanes = state.shape[1]
    tile = lanes // width
    full = jnp.concatenate([state] * tile, axis=0)
    row = lax.broadcasted_iota(jnp.int32, full.shape, 0) // order
    lane = lax.broadcasted_iota(jnp.int32, full.shape, 1) // width
    return jnp.where(row == lane, full, 0.0)


def split(value):
    high = value.astype(jnp.bfloat16)
    return high, (value - high.astype(jnp.float32)).astype(jnp.bfloat16)


def product3(a, b):
    (ah, al), (bh, bl) = split(a), split(b)
    dot = functools.partial(jnp.dot, preferred_element_type=jnp.float32)
    return dot(ah, bh) + (dot(ah, bl) + dot(al, bh))


def conv_kernel(
    width, q_ref, k_ref, v_ref, taps_ref, lags_ref, leave_ref, reach_ref, fade_ref, skip_ref,
    query_ref, base_ref, state_ref, toep_ref
):
    taps = taps_ref.shape[0]
    count, lanes = query_ref.shape
    order = state_ref.shape[0]
    tile = lanes // width

    def filtered(ref, which):
        value = ref[...].astype(jnp.float32)
        total = None
        for tap in range(taps):
            term = taps_ref[tap, which][None, :] * value[HALO - tap : HALO - tap + count]
            total = term if total is None else total + term
        return total

    query_ref[...] = filtered(q_ref, 0)
    gated = filtered(k_ref, 1) * filtered(v_ref, 2)
    lane = lax.broadcasted_iota(jnp.int32, (SUB, lanes), 1) // width
    row = lax.broadcasted_iota(jnp.int32, (tile * order, lanes), 0) // order
    diagonal = row == lax.broadcasted_iota(jnp.int32, (tile * order, lanes), 1) // width

    @pl.when(pl.program_id(1) == 0)
    def _():
        below = lax.broadcasted_iota(jnp.int32, (SUB, SUB), 0) >= lax.broadcasted_iota(
            jnp.int32, (SUB, SUB), 1
        )
        for g in range(tile):
            wide = jnp.broadcast_to(lags_ref[g : g + 1], (SUB, SUB))
            rolled = pltpu.roll(wide, 0, 1, stride=1, stride_axis=0)
            toep_ref[g * SUB : (g + 1) * SUB] = jnp.where(below, rolled, 0.0).astype(jnp.bfloat16)

    toep = toep_ref[...]
    state = jnp.zeros((tile * order, lanes), jnp.float32)
    for block in range(count // SUB):
        piece = gated[block * SUB : (block + 1) * SUB]
        wide = jnp.dot(toep, piece.astype(jnp.bfloat16), preferred_element_type=jnp.float32)
        local = skip_ref[...] * piece
        picked = wide[:SUB]
        for g in range(1, tile):
            picked = jnp.where(lane == g, wide[g * SUB : (g + 1) * SUB], picked)
        local = local + picked
        if block:
            local = local + product3(reach_ref[:SUB], state)
        base_ref[block * SUB : (block + 1) * SUB] = local
        fresh = product3(leave_ref[...], piece)
        state = fade_ref[...] * state + jnp.where(diagonal, fresh, 0.0)
    compact = state[:order]
    for g in range(1, tile):
        compact = compact + state[g * order : (g + 1) * order]
    state_ref[...] = compact


def convolved(proj, taps, lags, leave, reach, fade, skip, width, order, count):
    chans = skip.shape[1]
    lanes = min(LANES, chans)
    steps = chans // lanes
    tile = lanes // width
    segments, rows, _ = proj.shape
    return pl.pallas_call(
        functools.partial(conv_kernel, width),
        grid=(steps, segments),
        in_specs=[
            pl.BlockSpec((None, rows, lanes), lambda i, j: (j, 0, i)),
            pl.BlockSpec((None, rows, lanes), lambda i, j: (j, 0, steps + i)),
            pl.BlockSpec((None, rows, lanes), lambda i, j: (j, 0, 2 * steps + i)),
            pl.BlockSpec((taps.shape[0], 3, lanes), lambda i, j: (0, 0, i)),
            pl.BlockSpec((tile, SUB), lambda i, j: (i, 0)),
            pl.BlockSpec((tile * order, SUB), lambda i, j: (i, 0)),
            pl.BlockSpec((count, tile * order), lambda i, j: (0, i)),
            pl.BlockSpec((tile * order, 1), lambda i, j: (i, 0)),
            pl.BlockSpec((1, lanes), lambda i, j: (0, i)),
        ],
        out_specs=[
            pl.BlockSpec((None, count, lanes), lambda i, j: (j, 0, i)),
            pl.BlockSpec((None, count, lanes), lambda i, j: (j, 0, i)),
            pl.BlockSpec((None, order, lanes), lambda i, j: (j, 0, i)),
        ],
        out_shape=[
            jax.ShapeDtypeStruct((segments, count, chans), jnp.float32),
            jax.ShapeDtypeStruct((segments, count, chans), jnp.float32),
            jax.ShapeDtypeStruct((segments, order, chans), jnp.float32),
        ],
        scratch_shapes=[pltpu.VMEM((tile * SUB, SUB), jnp.bfloat16)],
        cost_estimate=pl.CostEstimate(
            flops=2 * count * chans * SUB * tile, bytes_accessed=count * chans * 20, transcendentals=0
        ),
        name="conv",
    )(proj, proj, proj, taps, lags, leave, reach, fade, skip)


def place():
    size, here = lax.axis_size("seq"), lax.axis_index("seq")
    return here // 4, lax.rem(here // 2, 2), lax.rem(here, 2), size // 4


def index_of(z, x, core):
    return z * 4 + x * 2 + core


def greet(peers):
    barrier = pltpu.get_barrier_semaphore()
    for peer in peers:
        pl.semaphore_signal(barrier, inc=1, device_id=peer, device_id_type=MESH)
    pl.semaphore_wait(barrier, len(peers))


def remote(source, target, send_sem, recv_sem, peer):
    return pltpu.make_async_remote_copy(
        src_ref=source,
        dst_ref=target,
        send_sem=send_sem,
        recv_sem=recv_sem,
        device_id=peer,
        device_id_type=MESH,
    )


def gather_kernel(
    own_ref, pieces_ref, out_ref, tok_ref, w_ref, wo_ref, local_sems,
    line_send, line_recv, pass_send, pass_recv, pair_send, pair_recv,
    tp_send, tp_recv, core_send, core_recv, early_send, early_recv,
    cols_send, cols_recv, swap_send, swap_recv,
):
    z, x, core, depth = place()
    parity = lax.rem(z, 2)
    n_tp, part = lax.axis_size("tp"), lax.axis_index("tp")
    mine = index_of(z, x, core)
    side = {"seq": index_of(z, 1 - x, core)}
    twin = {"seq": index_of(z, x, 1 - core)}

    def on_line(hop):
        there = z ^ hop[0]
        return there, (1 - core if hop[1] else core)

    hops = [(step, other) for step in range(depth) for other in range(2)][1:]
    peers = [side] + [
        {"seq": index_of(there, x, which)} for there, which in map(on_line, hops)
    ]
    tps = [{"tp": lax.rem(part + d, n_tp)} for d in range(1, n_tp)]
    greet(peers + tps)

    cols = own_ref.shape[1] // (2 * n_tp)

    def band(which, piece):
        return pl.ds(pl.multiple_of((2 * which + piece) * cols, cols), cols)

    own_slot, mate_slot = 2 * parity + core, 2 * (1 - parity) + core
    stay = [
        pltpu.make_async_copy(own_ref, tok_ref.at[own_slot], local_sems.at[0]),
        pltpu.make_async_copy(pieces_ref.at[own_slot], w_ref.at[mine], local_sems.at[1]),
    ]
    started = []

    def begin(*what):
        copy = remote(*what)
        copy.start()
        started.append(copy)
        return copy

    def to_line(hop):
        there, which = on_line(hop)
        index = 2 * hop[0] + hop[1]
        return begin(
            pieces_ref.at[2 * lax.rem(there, 2) + which], w_ref.at[mine],
            line_send.at[index], line_recv.at[index], {"seq": index_of(there, x, which)},
        )

    def to_pair(piece):
        where = tok_ref.at[own_slot, :, band(part, piece)]
        return begin(
            own_ref.at[:, band(part, piece)], where, pair_send.at[piece], pair_recv.at[piece],
            {"seq": index_of(z ^ 1, x, core)},
        )

    quarter = wo_ref.shape[1] // 4
    out_cols = wo_ref.shape[2]

    def quarter_rows(piece):
        return pl.ds(pl.multiple_of((2 * core + piece) * quarter, quarter), quarter)

    def columns(d, piece):
        target = lax.rem(part + d, n_tp)
        slot = 2 * (d - 1) + piece
        return begin(
            out_ref.at[quarter_rows(piece), pl.ds(pl.multiple_of(target * out_cols, out_cols), out_cols)],
            wo_ref.at[d - 1, quarter_rows(piece)],
            cols_send.at[slot], cols_recv.at[slot], tps[d - 1],
        )

    def swap(d, piece):
        slot = 2 * (d - 1) + piece
        where = wo_ref.at[d - 1, quarter_rows(piece)]
        return begin(where, where, swap_send.at[slot], swap_recv.at[slot], twin)

    paired = [to_pair(0)]
    first = begin(
        pieces_ref.at[own_slot], w_ref.at[mine], pass_send.at[0], pass_recv.at[0], side
    )
    line = {}
    for hop in hops[:2]:
        line[hop] = to_line(hop)
    paired.append(to_pair(1))
    for hop in hops[2:]:
        line[hop] = to_line(hop)
    moved = {(d, 0): columns(d, 0) for d in range(1, n_tp)}
    early = begin(own_ref, tok_ref.at[own_slot], early_send, early_recv, twin)
    for copy in stay:
        copy.start()

    forwards = []

    def hand_on(hop):
        index = 2 * hop[0] + hop[1]
        source = index_of(on_line(hop)[0], x, on_line(hop)[1])
        line[hop].wait_recv()
        forwards.append(begin(
            w_ref.at[source], w_ref.at[source], pass_send.at[index], pass_recv.at[index], side
        ))

    twins, across = [], {}

    def to_twin(which, piece, d):
        where = tok_ref.at[mate_slot, :, band(which, piece)]
        slot = 2 * d + piece
        twins.append(begin(where, where, core_send.at[slot], core_recv.at[slot], twin))

    def pair_on(piece):
        paired[piece].wait_recv()
        where = tok_ref.at[mate_slot, :, band(part, piece)]
        for d in range(1, n_tp):
            slot = 2 * (d - 1) + piece
            across[d, piece] = begin(
                where, where, tp_send.at[slot], tp_recv.at[slot], tps[d - 1]
            )
        to_twin(part, piece, 0)

    hand_on(hops[0])
    pair_on(0)
    hand_on(hops[1])
    hand_on(hops[3])
    pair_on(1)
    for d in range(1, n_tp):
        moved[d, 1] = columns(d, 1)
    hand_on(hops[2])
    for hop in hops[4:]:
        hand_on(hop)
    for piece in range(2):
        for d in range(1, n_tp):
            moved[d, piece].wait_recv()
            twins.append(swap(d, piece))
            across[d, piece].wait_recv()
            to_twin(lax.rem(part - d + n_tp, n_tp), piece, d)
    for copy in [first, early] + forwards + twins:
        copy.wait_recv()
    for copy in started:
        copy.wait_send()
    for copy in stay:
        copy.wait()


def gathered(own, pieces, w_out):
    size, n_tp = lax.axis_size("seq"), lax.axis_size("tp")
    line = size // 2
    anywhere = pl.BlockSpec(memory_space=pl.ANY)
    counts = [2, line, line, line, line, 2, 2] + [2 * n_tp] * 4 + [0, 0] + [2 * n_tp] * 4
    return pl.pallas_call(
        gather_kernel,
        out_shape=[
            jax.ShapeDtypeStruct((4,) + own.shape, own.dtype),
            jax.ShapeDtypeStruct((size,) + pieces.shape[1:], pieces.dtype),
            jax.ShapeDtypeStruct(
                (n_tp - 1, w_out.shape[0], w_out.shape[1] // n_tp), w_out.dtype
            ),
        ],
        in_specs=[anywhere] * 3,
        out_specs=[anywhere] * 3,
        scratch_shapes=[pltpu.SemaphoreType.DMA((n,) if n else ()) for n in counts],
        compiler_params=pltpu.CompilerParams(collective_id=0, has_side_effects=True),
        name="gather",
    )(own, pieces, w_out)


def share_kernel(own_ref, all_ref, send_sems, recv_sems):
    total = all_ref.shape[0]
    z, x, core, depth = place()
    here = (z // 2) * 2 + x

    def peer(d):
        there = lax.rem(here + d, total)
        return {"seq": index_of(2 * (there // 2) + lax.rem(z, 2), lax.rem(there, 2), core)}

    peers = [peer(d) for d in range(1, total)]
    greet(peers)
    copies = []
    for d in range(1, total):
        copy = remote(
            own_ref, all_ref.at[here], send_sems.at[d - 1], recv_sems.at[d - 1], peers[d - 1]
        )
        copy.start()
        copies.append(copy)
    all_ref[here] = own_ref[...]
    for copy in copies:
        copy.wait()


def shared(state):
    total = lax.axis_size("seq") // 4
    return pl.pallas_call(
        share_kernel,
        out_shape=jax.ShapeDtypeStruct((total,) + state.shape, state.dtype),
        in_specs=[pl.BlockSpec(memory_space=pltpu.VMEM)],
        out_specs=pl.BlockSpec(memory_space=pltpu.VMEM),
        scratch_shapes=[
            pltpu.SemaphoreType.DMA((total - 1,)),
            pltpu.SemaphoreType.DMA((total - 1,)),
        ],
        compiler_params=pltpu.CompilerParams(collective_id=1, has_side_effects=True),
        name="share",
    )(state)


def spread_kernel(mix_ref, full_ref, local_sem, send_sems, recv_sems, tp_send, tp_recv):
    z, x, core, _ = place()
    chans = mix_ref.shape[2]
    n_tp, part = lax.axis_size("tp"), lax.axis_index("tp")
    parity = lax.rem(z, 2)
    me = 2 * parity + core

    def peer(d):
        there = (z ^ (d // 2), (1 - core if d % 2 else core))
        return 2 * lax.rem(there[0], 2) + there[1], {"seq": index_of(there[0], x, there[1])}

    tps = [{"tp": lax.rem(part + d, n_tp)} for d in range(1, n_tp)]
    greet([peer(d)[1] for d in range(1, 4)] + tps)

    def at(slot, which):
        return full_ref.at[slot, :, pl.ds(pl.multiple_of(which * chans, chans), chans)]

    across = []

    def over(source, which, n):
        for d in range(1, n_tp):
            sem = 4 * (d - 1) + n
            copy = remote(source, at(d, which), tp_send.at[sem], tp_recv.at[sem], tps[d - 1])
            copy.start()
            across.append(copy)

    copies = []
    for d in (2, 3, 1):
        there, device = peer(d)
        copy = remote(
            mix_ref.at[there], at(0, me), send_sems.at[d - 1], recv_sems.at[d - 1], device
        )
        copy.start()
        copies.append((d, copy))
    over(mix_ref.at[me], me, 0)
    stay = pltpu.make_async_copy(mix_ref.at[me], at(0, me), local_sem)
    stay.start()
    for d, copy in copies[2:] + copies[:2]:
        copy.wait_recv()
        which = peer(d)[0]
        over(at(0, which), which, d)
    for _, copy in copies:
        copy.wait_send()
    for copy in across:
        copy.wait()
    stay.wait()


def spread(mix):
    n_tp = lax.axis_size("tp")
    roles, count, chans = mix.shape
    return pl.pallas_call(
        spread_kernel,
        out_shape=jax.ShapeDtypeStruct((n_tp, count, roles * chans), mix.dtype),
        in_specs=[pl.BlockSpec(memory_space=pltpu.VMEM)],
        out_specs=pl.BlockSpec(memory_space=pltpu.VMEM),
        scratch_shapes=[
            pltpu.SemaphoreType.DMA(()),
            pltpu.SemaphoreType.DMA((3,)),
            pltpu.SemaphoreType.DMA((3,)),
            pltpu.SemaphoreType.DMA((4 * n_tp,)),
            pltpu.SemaphoreType.DMA((4 * n_tp,)),
        ],
        compiler_params=pltpu.CompilerParams(collective_id=2, has_side_effects=True),
        name="spread",
    )(mix)


def mix_kernel(width, query_ref, base_ref, all_ref, weight_ref, reach_ref, mix_ref):
    order = all_ref.shape[1]
    entering = jnp.sum(all_ref[...] * weight_ref[...], axis=0)
    carried = product3(reach_ref[...], fanned(entering, width, order))
    mix_ref[...] = (query_ref[...] * (base_ref[...] + carried)).astype(mix_ref.dtype)


def mixed_of(query, base, everything, weight, reach, width):
    segments, count, chans = query.shape
    size, order, _ = everything.shape
    lanes = min(LANES, chans)
    cols = lanes // width * order
    return pl.pallas_call(
        functools.partial(mix_kernel, width),
        grid=(chans // lanes, segments),
        in_specs=[
            pl.BlockSpec((None, count, lanes), lambda i, j: (j, 0, i)),
            pl.BlockSpec((None, count, lanes), lambda i, j: (j, 0, i)),
            pl.BlockSpec((size, order, lanes), lambda i, j: (0, 0, i)),
            pl.BlockSpec((None, size, order, lanes), lambda i, j: (j, 0, 0, i)),
            pl.BlockSpec((count, cols), lambda i, j: (0, i)),
        ],
        out_specs=pl.BlockSpec((None, count, lanes), lambda i, j: (j, 0, i)),
        out_shape=jax.ShapeDtypeStruct((segments, count, chans), jnp.bfloat16),
        name="mix",
    )(query, base, everything, weight, reach)


def shards(tokens, w_in, short_taps, decay_rate, residue, skip_gain, w_out):
    count = tokens.shape[0]
    rows, _, all_chans = w_in.shape
    width = all_chans // decay_rate.shape[0]
    taps = short_taps.shape[0]
    z, x, core, depth = place()
    parity = lax.rem(z, 2)
    role = 2 * parity + core
    n_tp, part = lax.axis_size("tp"), lax.axis_index("tp")
    chans = all_chans // 4

    before = shifted_by(tokens[count - (taps - 1) :], "seq", 1)
    extended = jnp.concatenate(
        [jnp.zeros((HALO - (taps - 1), tokens.shape[1]), tokens.dtype), before, tokens], axis=0
    )
    pieces = w_in.reshape(rows, 3, 4, chans).transpose(2, 0, 1, 3).reshape(4, rows, 3 * chans)
    tok, weights, out_rows = gathered(extended, pieces, w_out)

    def own(array, axis):
        share = array.shape[axis] // 4
        return lax.dynamic_slice_in_dim(array, role * share, share, axis)

    short_taps, skip = own(short_taps, 2), own(skip_gain[None], 1)
    decay_rate, residue = own(decay_rate, 0), own(residue, 0)
    groups, order = decay_rate.shape
    weight_mode = residue * jnp.sqrt(2.0 * decay_rate / order)
    offsets = jnp.arange(SUB, dtype=jnp.float32)
    back = (-jnp.arange(SUB) % SUB).astype(jnp.float32)
    lags = jnp.einsum(
        "gm,gmd->gd",
        weight_mode,
        jnp.exp(-decay_rate[:, :, None] * back[None, None, :]),
        precision=HIGHEST,
    )
    rate = decay_rate.reshape(groups * order)
    leave = jnp.exp(-rate[:, None] * (SUB - 1.0 - offsets[None, :]))
    fade = jnp.exp(-rate * SUB)[:, None]
    positions = jnp.arange(count, dtype=jnp.float32)
    reach = weight_mode.reshape(groups * order)[None] * jnp.exp(
        -rate[None] * (positions[:, None] + 1.0)
    )
    by_mode = jnp.repeat(decay_rate.T, width, axis=1)
    slot = jnp.arange(4)
    own_block = index_of(2 * (z // 2) + slot // 2, x, slot % 2)
    team = jnp.arange(depth)[:, None]
    other_block = index_of(2 * (team // 2) + slot[None] // 2, team % 2, slot[None] % 2).reshape(-1)
    ahead = (own_block[:, None] - 1 - other_block[None, :])[:, :, None, None]
    weight = jnp.where(
        ahead >= 0, jnp.exp(-by_mode * (count * jnp.maximum(ahead, 0).astype(jnp.float32))), 0.0
    )

    proj = jnp.dot(
        tok.reshape(-1, tok.shape[2]),
        weights.reshape(-1, weights.shape[2]),
        preferred_element_type=jnp.float32,
    ).astype(jnp.bfloat16).reshape(4, -1, 3 * chans)
    query, base, final = convolved(
        proj, short_taps, lags, leave, reach, fade, skip, width, order, count
    )
    everything = shared(final).reshape(-1, order, chans)
    full = spread(mixed_of(query, base, everything, weight, reach, width))

    share = w_out.shape[1] // n_tp
    kept = lax.dynamic_slice_in_dim(w_out, part * share, share, axis=1)
    total = jnp.dot(full[0], kept, preferred_element_type=jnp.float32)
    for d in range(1, n_tp):
        total = total + jnp.dot(full[d], out_rows[d - 1], preferred_element_type=jnp.float32)
    return total.astype(jnp.bfloat16)


def solution(mesh):
    in_specs = (
        P("seq", None),
        P("seq", None, "tp"),
        P(None, None, "tp"),
        P("tp", None),
        P("tp", None),
        P("tp"),
        P("tp", None),
    )
    out_specs = P("seq", "tp")
    return jax.shard_map(shards, mesh=mesh, in_specs=in_specs, out_specs=out_specs, check_vma=False)
```

```python
import functools

import jax
import jax.numpy as jnp
from jax import lax
from jax.experimental import pallas as pl
from jax.experimental.pallas import tpu as pltpu
from jax.sharding import PartitionSpec as P

SUB = 128
LANES = 256
HALO = 16
MESH = pl.DeviceIdType.MESH
HIGHEST = lax.Precision.HIGHEST


def shifted_by(block, axis, distance):
    devices = range(lax.axis_size(axis))
    route = [(i - distance, i) for i in devices if i - distance in devices]
    return lax.ppermute(block, axis, route)


def fanned(state, width, order):
    lanes = state.shape[1]
    tile = lanes // width
    full = jnp.concatenate([state] * tile, axis=0)
    row = lax.broadcasted_iota(jnp.int32, full.shape, 0) // order
    lane = lax.broadcasted_iota(jnp.int32, full.shape, 1) // width
    return jnp.where(row == lane, full, 0.0)


def split(value):
    high = value.astype(jnp.bfloat16)
    return high, (value - high.astype(jnp.float32)).astype(jnp.bfloat16)


def product3(a, b):
    (ah, al), (bh, bl) = split(a), split(b)
    dot = functools.partial(jnp.dot, preferred_element_type=jnp.float32)
    return dot(ah, bh) + (dot(ah, bl) + dot(al, bh))


def conv_kernel(
    width, q_ref, k_ref, v_ref, taps_ref, lags_ref, leave_ref, reach_ref, fade_ref, skip_ref,
    query_ref, base_ref, state_ref, toep_ref
):
    taps = taps_ref.shape[0]
    count, lanes = query_ref.shape
    order = state_ref.shape[0]
    tile = lanes // width

    def filtered(ref, which):
        value = ref[...].astype(jnp.float32)
        total = None
        for tap in range(taps):
            term = taps_ref[tap, which][None, :] * value[HALO - tap : HALO - tap + count]
            total = term if total is None else total + term
        return total

    query_ref[...] = filtered(q_ref, 0)
    gated = filtered(k_ref, 1) * filtered(v_ref, 2)
    lane = lax.broadcasted_iota(jnp.int32, (SUB, lanes), 1) // width
    row = lax.broadcasted_iota(jnp.int32, (tile * order, lanes), 0) // order
    diagonal = row == lax.broadcasted_iota(jnp.int32, (tile * order, lanes), 1) // width

    @pl.when(pl.program_id(1) == 0)
    def _():
        below = lax.broadcasted_iota(jnp.int32, (SUB, SUB), 0) >= lax.broadcasted_iota(
            jnp.int32, (SUB, SUB), 1
        )
        for g in range(tile):
            wide = jnp.broadcast_to(lags_ref[g : g + 1], (SUB, SUB))
            rolled = pltpu.roll(wide, 0, 1, stride=1, stride_axis=0)
            toep_ref[g * SUB : (g + 1) * SUB] = jnp.where(below, rolled, 0.0).astype(jnp.bfloat16)

    toep = toep_ref[...]
    state = jnp.zeros((tile * order, lanes), jnp.float32)
    for block in range(count // SUB):
        piece = gated[block * SUB : (block + 1) * SUB]
        wide = jnp.dot(toep, piece.astype(jnp.bfloat16), preferred_element_type=jnp.float32)
        local = skip_ref[...] * piece
        picked = wide[:SUB]
        for g in range(1, tile):
            picked = jnp.where(lane == g, wide[g * SUB : (g + 1) * SUB], picked)
        local = local + picked
        if block:
            local = local + product3(reach_ref[:SUB], state)
        base_ref[block * SUB : (block + 1) * SUB] = local
        fresh = product3(leave_ref[...], piece)
        state = fade_ref[...] * state + jnp.where(diagonal, fresh, 0.0)
    compact = state[:order]
    for g in range(1, tile):
        compact = compact + state[g * order : (g + 1) * order]
    state_ref[...] = compact


def convolved(proj, taps, lags, leave, reach, fade, skip, width, order, count):
    chans = skip.shape[1]
    lanes = min(LANES, chans)
    steps = chans // lanes
    tile = lanes // width
    segments, rows, _ = proj.shape
    return pl.pallas_call(
        functools.partial(conv_kernel, width),
        grid=(steps, segments),
        in_specs=[
            pl.BlockSpec((None, rows, lanes), lambda i, j: (j, 0, i)),
            pl.BlockSpec((None, rows, lanes), lambda i, j: (j, 0, steps + i)),
            pl.BlockSpec((None, rows, lanes), lambda i, j: (j, 0, 2 * steps + i)),
            pl.BlockSpec((taps.shape[0], 3, lanes), lambda i, j: (0, 0, i)),
            pl.BlockSpec((tile, SUB), lambda i, j: (i, 0)),
            pl.BlockSpec((tile * order, SUB), lambda i, j: (i, 0)),
            pl.BlockSpec((count, tile * order), lambda i, j: (0, i)),
            pl.BlockSpec((tile * order, 1), lambda i, j: (i, 0)),
            pl.BlockSpec((1, lanes), lambda i, j: (0, i)),
        ],
        out_specs=[
            pl.BlockSpec((None, count, lanes), lambda i, j: (j, 0, i)),
            pl.BlockSpec((None, count, lanes), lambda i, j: (j, 0, i)),
            pl.BlockSpec((None, order, lanes), lambda i, j: (j, 0, i)),
        ],
        out_shape=[
            jax.ShapeDtypeStruct((segments, count, chans), jnp.float32),
            jax.ShapeDtypeStruct((segments, count, chans), jnp.float32),
            jax.ShapeDtypeStruct((segments, order, chans), jnp.float32),
        ],
        scratch_shapes=[pltpu.VMEM((tile * SUB, SUB), jnp.bfloat16)],
        cost_estimate=pl.CostEstimate(
            flops=2 * count * chans * SUB * tile, bytes_accessed=count * chans * 20, transcendentals=0
        ),
        name="conv",
    )(proj, proj, proj, taps, lags, leave, reach, fade, skip)


def place():
    size, here = lax.axis_size("seq"), lax.axis_index("seq")
    return here // 4, lax.rem(here // 2, 2), lax.rem(here, 2), size // 4


def index_of(z, x, core):
    return z * 4 + x * 2 + core


def greet(peers):
    barrier = pltpu.get_barrier_semaphore()
    for peer in peers:
        pl.semaphore_signal(barrier, inc=1, device_id=peer, device_id_type=MESH)
    pl.semaphore_wait(barrier, len(peers))


def remote(source, target, send_sem, recv_sem, peer):
    return pltpu.make_async_remote_copy(
        src_ref=source,
        dst_ref=target,
        send_sem=send_sem,
        recv_sem=recv_sem,
        device_id=peer,
        device_id_type=MESH,
    )


def gather_kernel(
    own_ref, halo_ref, pieces_ref, out_ref, tok_ref, w_ref, wo_ref, held_ref, held_w_ref, local_sems,
    line_send, line_recv, pass_send, pass_recv, pair_send, pair_recv,
    tp_send, tp_recv, core_send, core_recv, early_send, early_recv,
    cols_send, cols_recv, swap_send, swap_recv, halo_send, halo_recv,
):
    z, x, core, depth = place()
    parity = lax.rem(z, 2)
    n_tp, part = lax.axis_size("tp"), lax.axis_index("tp")
    mine = index_of(z, x, core)
    side = {"seq": index_of(z, 1 - x, core)}
    twin = {"seq": index_of(z, x, 1 - core)}

    def on_line(hop):
        there = z ^ hop[0]
        return there, (1 - core if hop[1] else core)

    hops = [(step, other) for step in range(depth) for other in range(2)][1:]
    peers = [side] + [
        {"seq": index_of(there, x, which)} for there, which in map(on_line, hops)
    ]
    tps = [{"tp": lax.rem(part + d, n_tp)} for d in range(1, n_tp)]
    greet(peers + tps)

    cols = own_ref.shape[1] // (2 * n_tp)

    def band(which, piece):
        return pl.ds(pl.multiple_of((2 * which + piece) * cols, cols), cols)

    own_slot, mate_slot = 2 * parity + core, 2 * (1 - parity) + core
    body = pl.ds(HALO, own_ref.shape[0])
    head = pl.ds(0, HALO)
    taken = [
        pltpu.make_async_copy(own_ref, held_ref.at[body], local_sems.at[0]),
        pltpu.make_async_copy(halo_ref, held_ref.at[head], local_sems.at[1]),
        pltpu.make_async_copy(pieces_ref.at[own_slot], held_w_ref, local_sems.at[2]),
    ]
    stay = [
        pltpu.make_async_copy(held_ref, tok_ref.at[own_slot], local_sems.at[3]),
        pltpu.make_async_copy(held_w_ref, w_ref.at[mine], local_sems.at[4]),
    ]
    for copy in taken:
        copy.start()
    started = []

    def begin(*what):
        copy = remote(*what)
        copy.start()
        started.append(copy)
        return copy

    def to_line(hop):
        there, which = on_line(hop)
        index = 2 * hop[0] + hop[1]
        return begin(
            pieces_ref.at[2 * lax.rem(there, 2) + which], w_ref.at[mine],
            line_send.at[index], line_recv.at[index], {"seq": index_of(there, x, which)},
        )

    def to_pair(piece):
        where = tok_ref.at[own_slot, body, band(part, piece)]
        return begin(
            own_ref.at[:, band(part, piece)], where, pair_send.at[piece], pair_recv.at[piece],
            {"seq": index_of(z ^ 1, x, core)},
        )

    quarter = wo_ref.shape[1] // 4
    out_cols = wo_ref.shape[2]

    def quarter_rows(piece):
        return pl.ds(pl.multiple_of((2 * core + piece) * quarter, quarter), quarter)

    def columns(d, piece):
        target = lax.rem(part + d, n_tp)
        slot = 2 * (d - 1) + piece
        return begin(
            out_ref.at[quarter_rows(piece), pl.ds(pl.multiple_of(target * out_cols, out_cols), out_cols)],
            wo_ref.at[d - 1, quarter_rows(piece)],
            cols_send.at[slot], cols_recv.at[slot], tps[d - 1],
        )

    def swap(d, piece):
        slot = 2 * (d - 1) + piece
        where = wo_ref.at[d - 1, quarter_rows(piece)]
        return begin(where, where, swap_send.at[slot], swap_recv.at[slot], twin)

    paired = [to_pair(0)]
    first = begin(
        pieces_ref.at[own_slot], w_ref.at[mine], pass_send.at[0], pass_recv.at[0], side
    )
    line = {}
    for hop in hops[:2]:
        line[hop] = to_line(hop)
    paired.append(to_pair(1))
    for hop in hops[2:]:
        line[hop] = to_line(hop)
    moved = {(d, 0): columns(d, 0) for d in range(1, n_tp)}
    early = begin(own_ref, tok_ref.at[own_slot, body], early_send, early_recv, twin)
    heads = []
    for n, hop in enumerate(hops[:3]):
        there, which = on_line(hop)
        heads.append(begin(
            halo_ref, tok_ref.at[own_slot, head], halo_send.at[n], halo_recv.at[n],
            {"seq": index_of(there, x, which)},
        ))
    for copy in taken:
        copy.wait()
    for copy in stay:
        copy.start()

    forwards = []

    def hand_on(hop):
        index = 2 * hop[0] + hop[1]
        source = index_of(on_line(hop)[0], x, on_line(hop)[1])
        line[hop].wait_recv()
        forwards.append(begin(
            w_ref.at[source], w_ref.at[source], pass_send.at[index], pass_recv.at[index], side
        ))

    twins, across = [], {}

    def to_twin(which, piece, d):
        where = tok_ref.at[mate_slot, body, band(which, piece)]
        slot = 2 * d + piece
        twins.append(begin(where, where, core_send.at[slot], core_recv.at[slot], twin))

    def pair_on(piece):
        paired[piece].wait_recv()
        where = tok_ref.at[mate_slot, body, band(part, piece)]
        for d in range(1, n_tp):
            slot = 2 * (d - 1) + piece
            across[d, piece] = begin(
                where, where, tp_send.at[slot], tp_recv.at[slot], tps[d - 1]
            )
        to_twin(part, piece, 0)

    hand_on(hops[0])
    pair_on(0)
    hand_on(hops[1])
    hand_on(hops[3])
    pair_on(1)
    for d in range(1, n_tp):
        moved[d, 1] = columns(d, 1)
    hand_on(hops[2])
    for hop in hops[4:]:
        hand_on(hop)
    for piece in range(2):
        for d in range(1, n_tp):
            moved[d, piece].wait_recv()
            twins.append(swap(d, piece))
            across[d, piece].wait_recv()
            to_twin(lax.rem(part - d + n_tp, n_tp), piece, d)
    for copy in [first, early] + heads + forwards + twins:
        copy.wait_recv()
    for copy in started:
        copy.wait_send()
    for copy in stay:
        copy.wait()


def gathered(own, halo, pieces, w_out):
    size, n_tp = lax.axis_size("seq"), lax.axis_size("tp")
    line = size // 2
    anywhere = pl.BlockSpec(memory_space=pl.ANY)
    counts = [5, line, line, line, line, 2, 2] + [2 * n_tp] * 4 + [0, 0] + [2 * n_tp] * 4 + [3, 3]
    return pl.pallas_call(
        gather_kernel,
        out_shape=[
            jax.ShapeDtypeStruct((4, HALO + own.shape[0], own.shape[1]), own.dtype),
            jax.ShapeDtypeStruct((size,) + pieces.shape[1:], pieces.dtype),
            jax.ShapeDtypeStruct(
                (n_tp - 1, w_out.shape[0], w_out.shape[1] // n_tp), w_out.dtype
            ),
        ],
        in_specs=[anywhere] * 4,
        out_specs=[anywhere] * 3,
        scratch_shapes=[
            pltpu.VMEM((HALO + own.shape[0], own.shape[1]), own.dtype),
            pltpu.VMEM(pieces.shape[1:], pieces.dtype),
        ]
        + [pltpu.SemaphoreType.DMA((n,) if n else ()) for n in counts],
        compiler_params=pltpu.CompilerParams(collective_id=0, has_side_effects=True),
        name="gather",
    )(own, halo, pieces, w_out)


def share_kernel(own_ref, all_ref, send_sems, recv_sems):
    total = all_ref.shape[0]
    z, x, core, depth = place()
    here = (z // 2) * 2 + x

    def peer(d):
        there = lax.rem(here + d, total)
        return {"seq": index_of(2 * (there // 2) + lax.rem(z, 2), lax.rem(there, 2), core)}

    peers = [peer(d) for d in range(1, total)]
    greet(peers)
    copies = []
    for d in range(1, total):
        copy = remote(
            own_ref, all_ref.at[here], send_sems.at[d - 1], recv_sems.at[d - 1], peers[d - 1]
        )
        copy.start()
        copies.append(copy)
    all_ref[here] = own_ref[...]
    for copy in copies:
        copy.wait()


def shared(state):
    total = lax.axis_size("seq") // 4
    return pl.pallas_call(
        share_kernel,
        out_shape=jax.ShapeDtypeStruct((total,) + state.shape, state.dtype),
        in_specs=[pl.BlockSpec(memory_space=pltpu.VMEM)],
        out_specs=pl.BlockSpec(memory_space=pltpu.VMEM),
        scratch_shapes=[
            pltpu.SemaphoreType.DMA((total - 1,)),
            pltpu.SemaphoreType.DMA((total - 1,)),
        ],
        compiler_params=pltpu.CompilerParams(collective_id=1, has_side_effects=True),
        name="share",
    )(state)


def spread_kernel(mix_ref, full_ref, local_sem, send_sems, recv_sems, tp_send, tp_recv):
    z, x, core, _ = place()
    chans = mix_ref.shape[2]
    n_tp, part = lax.axis_size("tp"), lax.axis_index("tp")
    parity = lax.rem(z, 2)
    me = 2 * parity + core

    def peer(d):
        there = (z ^ (d // 2), (1 - core if d % 2 else core))
        return 2 * lax.rem(there[0], 2) + there[1], {"seq": index_of(there[0], x, there[1])}

    tps = [{"tp": lax.rem(part + d, n_tp)} for d in range(1, n_tp)]
    greet([peer(d)[1] for d in range(1, 4)] + tps)

    def at(slot, which):
        return full_ref.at[slot, :, pl.ds(pl.multiple_of(which * chans, chans), chans)]

    across = []

    def over(source, which, n):
        for d in range(1, n_tp):
            sem = 4 * (d - 1) + n
            copy = remote(source, at(d, which), tp_send.at[sem], tp_recv.at[sem], tps[d - 1])
            copy.start()
            across.append(copy)

    copies = []
    for d in (2, 3, 1):
        there, device = peer(d)
        copy = remote(
            mix_ref.at[there], at(0, me), send_sems.at[d - 1], recv_sems.at[d - 1], device
        )
        copy.start()
        copies.append((d, copy))
    over(mix_ref.at[me], me, 0)
    stay = pltpu.make_async_copy(mix_ref.at[me], at(0, me), local_sem)
    stay.start()
    for d, copy in copies[2:] + copies[:2]:
        copy.wait_recv()
        which = peer(d)[0]
        over(at(0, which), which, d)
    for _, copy in copies:
        copy.wait_send()
    for copy in across:
        copy.wait()
    stay.wait()


def spread(mix):
    n_tp = lax.axis_size("tp")
    roles, count, chans = mix.shape
    return pl.pallas_call(
        spread_kernel,
        out_shape=jax.ShapeDtypeStruct((n_tp, count, roles * chans), mix.dtype),
        in_specs=[pl.BlockSpec(memory_space=pltpu.VMEM)],
        out_specs=pl.BlockSpec(memory_space=pltpu.VMEM),
        scratch_shapes=[
            pltpu.SemaphoreType.DMA(()),
            pltpu.SemaphoreType.DMA((3,)),
            pltpu.SemaphoreType.DMA((3,)),
            pltpu.SemaphoreType.DMA((4 * n_tp,)),
            pltpu.SemaphoreType.DMA((4 * n_tp,)),
        ],
        compiler_params=pltpu.CompilerParams(collective_id=2, has_side_effects=True),
        name="spread",
    )(mix)


def mix_kernel(width, query_ref, base_ref, all_ref, weight_ref, reach_ref, mix_ref):
    order = all_ref.shape[1]
    entering = jnp.sum(all_ref[...] * weight_ref[...], axis=0)
    carried = product3(reach_ref[...], fanned(entering, width, order))
    mix_ref[...] = (query_ref[...] * (base_ref[...] + carried)).astype(mix_ref.dtype)


def mixed_of(query, base, everything, weight, reach, width):
    segments, count, chans = query.shape
    size, order, _ = everything.shape
    lanes = min(LANES, chans)
    cols = lanes // width * order
    return pl.pallas_call(
        functools.partial(mix_kernel, width),
        grid=(chans // lanes, segments),
        in_specs=[
            pl.BlockSpec((None, count, lanes), lambda i, j: (j, 0, i)),
            pl.BlockSpec((None, count, lanes), lambda i, j: (j, 0, i)),
            pl.BlockSpec((size, order, lanes), lambda i, j: (0, 0, i)),
            pl.BlockSpec((None, size, order, lanes), lambda i, j: (j, 0, 0, i)),
            pl.BlockSpec((count, cols), lambda i, j: (0, i)),
        ],
        out_specs=pl.BlockSpec((None, count, lanes), lambda i, j: (j, 0, i)),
        out_shape=jax.ShapeDtypeStruct((segments, count, chans), jnp.bfloat16),
        name="mix",
    )(query, base, everything, weight, reach)


def shards(tokens, w_in, short_taps, decay_rate, residue, skip_gain, w_out):
    count = tokens.shape[0]
    rows, _, all_chans = w_in.shape
    width = all_chans // decay_rate.shape[0]
    taps = short_taps.shape[0]
    z, x, core, depth = place()
    parity = lax.rem(z, 2)
    role = 2 * parity + core
    n_tp, part = lax.axis_size("tp"), lax.axis_index("tp")
    chans = all_chans // 4

    before = shifted_by(tokens[count - (taps - 1) :], "seq", 1)
    halo = jnp.pad(before, ((HALO - (taps - 1), 0), (0, 0)))
    pieces = w_in.reshape(rows, 3, 4, chans).transpose(2, 0, 1, 3).reshape(4, rows, 3 * chans)
    tok, weights, out_rows = gathered(tokens, halo, pieces, w_out)

    def own(array, axis):
        share = array.shape[axis] // 4
        return lax.dynamic_slice_in_dim(array, role * share, share, axis)

    short_taps, skip = own(short_taps, 2), own(skip_gain[None], 1)
    decay_rate, residue = own(decay_rate, 0), own(residue, 0)
    groups, order = decay_rate.shape
    weight_mode = residue * jnp.sqrt(2.0 * decay_rate / order)
    offsets = jnp.arange(SUB, dtype=jnp.float32)
    back = (-jnp.arange(SUB) % SUB).astype(jnp.float32)
    lags = jnp.einsum(
        "gm,gmd->gd",
        weight_mode,
        jnp.exp(-decay_rate[:, :, None] * back[None, None, :]),
        precision=HIGHEST,
    )
    rate = decay_rate.reshape(groups * order)
    leave = jnp.exp(-rate[:, None] * (SUB - 1.0 - offsets[None, :]))
    fade = jnp.exp(-rate * SUB)[:, None]
    positions = jnp.arange(count, dtype=jnp.float32)
    reach = weight_mode.reshape(groups * order)[None] * jnp.exp(
        -rate[None] * (positions[:, None] + 1.0)
    )
    by_mode = jnp.repeat(decay_rate.T, width, axis=1)
    slot = jnp.arange(4)
    own_block = index_of(2 * (z // 2) + slot // 2, x, slot % 2)
    team = jnp.arange(depth)[:, None]
    other_block = index_of(2 * (team // 2) + slot[None] // 2, team % 2, slot[None] % 2).reshape(-1)
    ahead = (own_block[:, None] - 1 - other_block[None, :])[:, :, None, None]
    weight = jnp.where(
        ahead >= 0, jnp.exp(-by_mode * (count * jnp.maximum(ahead, 0).astype(jnp.float32))), 0.0
    )

    proj = jnp.dot(
        tok.reshape(-1, tok.shape[2]),
        weights.reshape(-1, weights.shape[2]),
        preferred_element_type=jnp.float32,
    ).astype(jnp.bfloat16).reshape(4, -1, 3 * chans)
    query, base, final = convolved(
        proj, short_taps, lags, leave, reach, fade, skip, width, order, count
    )
    everything = shared(final).reshape(-1, order, chans)
    full = spread(mixed_of(query, base, everything, weight, reach, width))

    share = w_out.shape[1] // n_tp
    kept = lax.dynamic_slice_in_dim(w_out, part * share, share, axis=1)
    total = jnp.dot(full[0], kept, preferred_element_type=jnp.float32)
    for d in range(1, n_tp):
        total = total + jnp.dot(full[d], out_rows[d - 1], preferred_element_type=jnp.float32)
    return total.astype(jnp.bfloat16)


def solution(mesh):
    in_specs = (
        P("seq", None),
        P("seq", None, "tp"),
        P(None, None, "tp"),
        P("tp", None),
        P("tp", None),
        P("tp"),
        P("tp", None),
    )
    out_specs = P("seq", "tp")
    return jax.shard_map(shards, mesh=mesh, in_specs=in_specs, out_specs=out_specs, check_vma=False)
```
